128 devices in a mesh: leaf: 32 (over y, x, core), probe: 4 (over z).
Axes of the slice: x: 4, y: 4, z: 4, core: 2. Of those that a mesh axis runs over, the one named last changes fastest.
Arguments:
- points: bfloat16 [131072, 2048], P('leaf', 'probe'), parts along dimension 1, may hold values from -6 to 6
- leaf_basis: bfloat16 [512, 64, 256], P('leaf'), may hold values from -0.375 to 0.375
- local_transfer: bfloat16 [960, 4096], P('leaf'), may hold values from -0.5 to 0.5
- top_transfer: bfloat16 [62, 4096], replicated, may hold values from -0.5 to 0.5
- sources: int32 [32736], P('leaf'), may hold values from 0 to 511, as said below
- couplings: bfloat16 [32736, 4096], P('leaf'), as said below
Outputs:
- coupled: bfloat16 [992, 64, 2048], P('leaf', None, 'probe'), parts along dimension 2
- ancestors: bfloat16 [32, 5, 64, 2048], P('leaf', None, None, 'probe'), parts along dimension 3
The draws below stay inside these ranges and needn't reach their ends.
There are 4 independent parts, one for each index of `probe`. The reference program is written for one: setup_inputs(seed, part) draws one part's arguments, and reference() takes and returns one part's arrays. A program takes and returns all parts, laid end to end along the dimension named above; an argument that names none is the same for every part. Nothing has to cross between parts.
Inputs may be any that keep to these rules, and one draw needn't show every extreme that they name: `sources`: each entry names a cluster of its target's level lying in the target's subtree or in one of the two subtrees on either side; the entries of one target are distinct. `couplings`: tiles of level h have entries of deviation (3 * 64 * 16 / 2^h)^(-1/2).
All inputs are finite; a program needn't handle non-finite values.
Results may differ from the reference program's by a relative error of at most 0.0095.
Values may be sent and summed in bfloat16 or wider, within the bound.
No kernel may reach another device: no remote copies, remote signals or barrier semaphores. Data moves between devices by JAX's collectives and lax.ppermute only.
A program may use at most 128 MiB of HBM per device.

```python
from functools import partial
import jax
import jax.numpy as jnp
from jax import lax

LEAF = 256
RANK = 64
PROBES = 512
LOCAL = 5
TOP = 5
LEAF_DEV = 16
NLEAF = 512
POINTS = 131072
TARGETS_DEV = 31
LINKS_DEV = 30
PAIRS_DEV = 1023
TOP_LINKS = 62
N_LEAF = 32


def draw_sources(key, part):
    pieces = []
    for height in range(LOCAL):
        number = LEAF_DEV >> height
        breadth = 5 * number
        clusters = number * N_LEAF
        scores = jax.random.randint(jax.random.fold_in(key, height), (N_LEAF, number, breadth), 0, 2 ** 20)
        columns = jnp.arange(breadth, dtype=jnp.int32)
        anchor = (jnp.arange(N_LEAF, dtype=jnp.int32) - 2) * number
        candidates = anchor[:, None, None] + columns[None, None, :]
        inside = (candidates >= 0) & (candidates < clusters)
        ranked_keys = scores * (8 * number) + columns + jnp.where(inside, 0, 2 ** 29)
        ranked = jnp.argsort(ranked_keys, axis=-1)[:, :, :3 * number]
        chosen = jnp.take_along_axis(candidates, ranked, axis=-1)
        pieces.append(chosen.reshape(N_LEAF, 3 * number * number))
    return jnp.concatenate(pieces, axis=1).reshape(N_LEAF * PAIRS_DEV).astype(jnp.int32)


def draw_couplings(key, part):
    pieces = []
    for height in range(LOCAL):
        number = LEAF_DEV >> height
        spread = (3.0 * RANK * number) ** (-0.5)
        extent = (N_LEAF, 3 * number * number, RANK * RANK)
        level_key = jax.random.fold_in(key, 100 + height)
        values = jax.random.normal(level_key, extent, jnp.float32)
        pieces.append(values * spread)
    return jnp.concatenate(pieces, axis=1).reshape(N_LEAF * PAIRS_DEV, RANK * RANK).astype(jnp.bfloat16)


def shard_levels(stream_key, shape, cuts, least, top_value):
    factor_of, own = 1.0, jax.random.fold_in(stream_key, 6)
    for axis_at, shards_of in cuts:
        heights = jnp.exp(jax.random.uniform(jax.random.fold_in(own, axis_at), (shards_of,), jnp.float32, least / len(cuts), top_value / len(cuts)))
        factor_of = factor_of * jnp.repeat(heights, shape[axis_at] // shards_of).reshape([-1 if axis == axis_at else 1 for axis in range(len(shape))])
    return factor_of


def normal_values(stream_key, dims, scale, bound, cuts=(), held_as=jnp.bfloat16):
    level = shard_levels(stream_key, dims, cuts, -0.22, 0.18) if cuts else 1.0
    values = jax.random.normal(stream_key, dims, jnp.float32) * scale * level
    return jnp.minimum(jnp.maximum(values, -bound), bound).astype(held_as)


def setup_inputs(seed: int = 0, part: int = 0) -> dict:
    keys = jax.random.split(jax.random.key(seed), 7)
    own_keys = jax.random.split(jax.random.fold_in(keys[6], part), 7)
    return {
        "points": normal_values(own_keys[0], (POINTS, PROBES), 1.0, 6.0, ((0, 32),)),
        "leaf_basis": normal_values(keys[1], (NLEAF, RANK, LEAF), LEAF ** -0.5, 0.375, ((0, 32),)),
        "local_transfer": normal_values(keys[2], (LINKS_DEV * N_LEAF, RANK * RANK), (2 * RANK) ** -0.5, 0.5, ((0, 32),)),
        "top_transfer": normal_values(keys[3], (TOP_LINKS, RANK * RANK), (2 * RANK) ** -0.5, 0.5),
        "sources": draw_sources(jax.random.fold_in(keys[6], 71), part),
        "couplings": draw_couplings(jax.random.fold_in(keys[6], 71), part),
    }


def lift_level(children, matrices):
    products = jnp.einsum("cab,cap->cbp", matrices.astype(jnp.float32).reshape(-1, RANK, RANK), children.astype(jnp.float32), precision=lax.Precision.HIGHEST)
    return products.reshape(-1, 2, RANK, PROBES).sum(axis=1)


def couple_block(operands, level_moments, number):
    block_sources, block_tiles = operands
    picked = jnp.take(level_moments, block_sources, axis=0).astype(jnp.float32).reshape(number, 3 * number, RANK, PROBES)
    matrices = block_tiles.astype(jnp.float32).reshape(number, 3 * number, RANK, RANK)
    summed = jnp.einsum("tkab,tkap->tbp", matrices, picked, precision=lax.Precision.HIGHEST)
    return summed.astype(jnp.bfloat16)


def reference(points, leaf_basis, local_transfer, top_transfer, sources, couplings):
    blocks = points.reshape(NLEAF, LEAF, PROBES).astype(jnp.float32)
    first = jnp.einsum("jrl,jlp->jrp", leaf_basis.astype(jnp.float32), blocks, precision=lax.Precision.HIGHEST)
    moments = [first.astype(jnp.bfloat16)]
    link_rows = local_transfer.reshape(N_LEAF, LINKS_DEV, RANK * RANK)
    cursor = 0
    for height in range(1, LOCAL):
        number = LEAF_DEV >> (height - 1)
        matrices = link_rows[:, cursor:cursor + number].reshape(N_LEAF * number, RANK * RANK)
        moments.append(lift_level(moments[-1], matrices).astype(jnp.bfloat16))
        cursor += number
    source_rows = sources.reshape(N_LEAF, PAIRS_DEV)
    tile_rows = couplings.reshape(N_LEAF, PAIRS_DEV, RANK * RANK)
    outputs = []
    cursor = 0
    for height in range(LOCAL):
        number = LEAF_DEV >> height
        entries = 3 * number * number
        worker = partial(couple_block, level_moments=moments[height], number=number)
        outputs.append(lax.map(worker, (source_rows[:, cursor:cursor + entries], tile_rows[:, cursor:cursor + entries])))
        cursor += entries
    coupled = jnp.concatenate(outputs, axis=1).reshape(N_LEAF * TARGETS_DEV, RANK, PROBES)
    current = moments[LOCAL - 1]
    ladder = []
    cursor = 0
    for height in range(TOP):
        clusters = current.shape[0]
        current = lift_level(current, top_transfer[cursor:cursor + clusters]).astype(jnp.bfloat16)
        cursor += clusters
        ladder.append(jnp.repeat(current, 2 ** (height + 1), axis=0))
    ancestors = jnp.stack(ladder, axis=1)
    return coupled, ancestors
```

```python
import jax
import jax.numpy as jnp
from jax import lax
from jax.experimental import pallas as pl
from jax.experimental.pallas import tpu as pltpu
from jax.sharding import PartitionSpec as P

LEAF = 256
RANK = 64
PROBES = 512
LOCAL = 5
LEAF_DEV = 16
GROUPS = 32
HALF = 32
BF = jnp.bfloat16
F32 = jnp.float32
COUNTS = (16, 8, 4, 2, 1)
LIFT_ROWS = (0, 512, 768, 896)


def iotas(rows, columns):
    shape = (rows, columns)
    return (
        lax.broadcasted_iota(jnp.int32, shape, 0),
        lax.broadcasted_iota(jnp.int32, shape, 1),
    )


def natural(rank):
    return (rank & 31) * 2 + (rank >> 5)


def ones_where(mask):
    return jnp.where(mask, 1.0, 0.0).astype(BF)


def rank_order():
    row, column = iotas(RANK, RANK)
    return ones_where(column == natural(row))


def rank_order_pair():
    row, column = iotas(2 * RANK, 2 * RANK)
    return ones_where(column == (row & 64) + natural(row & 63))


def identity(size):
    row, column = iotas(size, size)
    return ones_where(row == column)


def group_order():
    row, column = iotas(256, 256)
    return ones_where(column == (row & 15) * 16 + (row >> 4))


def dot(left, right):
    return jnp.dot(left, right, preferred_element_type=F32)


def dot_nt(left, right):
    return lax.dot_general(left, right, (((1,), (1,)), ((), ())), preferred_element_type=F32)


def regrouped(block, order):
    halves = [
        jnp.concatenate(
            [block[:, (16 * half + g) * 128 : (16 * half + g + 1) * 128] for g in range(16)], axis=0
        )
        for half in range(2)
    ]
    return dot(order, jnp.concatenate(halves, axis=1)).astype(BF)


def tile_rows(regroup):
    pieces = []
    for entry in range(16):
        rows = slice(16 * entry, 16 * entry + 16)
        pieces.append(regroup[rows, :128])
        pieces.append(regroup[rows, 128:])
    return jnp.concatenate(pieces, axis=0)


def first_kernel(points_hbm, basis_hbm, links_hbm, out_ref, points_ref, basis_ref, links_ref, sems):
    links_copy = pltpu.make_async_copy(links_hbm, links_ref, sems.at[9])
    links_copy.start()
    basis_copy = pltpu.make_async_copy(basis_hbm, basis_ref, sems.at[8])
    basis_copy.start()
    copies = []
    for k in range(8):
        rows = pl.ds(512 * k, 512)
        copies.append(pltpu.make_async_copy(points_hbm.at[rows], points_ref.at[rows], sems.at[k]))
        copies[-1].start()
    order = group_order()
    flip = rank_order_pair()
    ranks = rank_order()
    links_copy.wait()
    high = jnp.concatenate([links_ref[16:30, :], jnp.zeros((2, 4096), BF)], axis=0)
    for number, block in enumerate((links_ref[0:16, :], high)):
        tiles = tile_rows(regrouped(block, order))
        out_ref[1024 + 128 * number : 1152 + 128 * number, :] = dot_nt(flip, tiles).astype(BF)
    basis_copy.wait()
    for k in range(8):
        basis = jnp.concatenate([basis_ref[2 * k], basis_ref[2 * k + 1]], axis=1)
        basis = dot(ranks, basis).astype(BF)
        copies[k].wait()
        for j in range(2):
            at = 512 * k + LEAF * j
            moment = dot(basis[:, LEAF * j : LEAF * (j + 1)], points_ref[at : at + LEAF, :]).astype(BF)
            to = (2 * k + j) * HALF
            out_ref[to : to + HALF, :] = moment[:HALF]
            out_ref[512 + to : 512 + to + HALF, :] = moment[HALF:]


VMEM_SPEC = pl.BlockSpec(memory_space=pltpu.VMEM)
HBM_SPEC = pl.BlockSpec(memory_space=pl.ANY)


def on_chip(value):
    return pltpu.with_memory_space_constraint(value, pltpu.VMEM)


def off_chip(value):
    return pltpu.with_memory_space_constraint(value, pltpu.HBM)


def limit(mebibytes):
    return pltpu.CompilerParams(vmem_limit_bytes=mebibytes << 20)


def first_moments(points, leaf_basis, local_transfer):
    return pl.pallas_call(
        first_kernel,
        in_specs=[HBM_SPEC] * 3,
        out_specs=VMEM_SPEC,
        out_shape=pltpu.VMEM((1280, PROBES), BF),
        scratch_shapes=[
            pltpu.VMEM((4096, PROBES), BF),
            pltpu.VMEM((LEAF_DEV, RANK, LEAF), BF),
            pltpu.VMEM((30, 4096), BF),
            pltpu.SemaphoreType.DMA((10,)),
        ],
        compiler_params=limit(10),
        name="first_moments",
    )(off_chip(points), off_chip(leaf_basis), off_chip(local_transfer))


def lift_into(packet, upper):
    low_side = lax.broadcasted_iota(jnp.int32, (RANK, 128), 1) < 64
    zero = jnp.zeros((RANK, 128), BF)

    def pair_of_targets(links, lanes, source, start, stride):
        total = None
        for side in range(2):
            left = packet[links + RANK * side : links + RANK * (side + 1), lanes : lanes + 128]
            left = jnp.concatenate(
                [jnp.where(low_side, left, zero), jnp.where(low_side, zero, left)], axis=0
            )
            begin = start + stride * side
            product = dot(left, source[begin : begin + 128, :])
            total = product if total is None else total + product
        return total.astype(BF)

    def keep(moment, base, count, first):
        for j in range(2):
            for side in range(2):
                at = base + side * count * HALF + (first + j) * HALF
                upper[at : at + HALF, :] = moment[j * RANK + side * HALF : j * RANK + (side + 1) * HALF]

    for u in range(4):
        keep(pair_of_targets(1024, 128 * u, packet, 128 * u, 512), 0, 8, 2 * u)
    for u in range(2):
        keep(pair_of_targets(1152, 128 * u, upper, 128 * u, 256), 512, 4, 2 * u)
    keep(pair_of_targets(1152, 256, upper, 512, 128), 768, 2, 0)
    total = None
    for side in range(2):
        left = packet[1152 + RANK * side : 1152 + RANK * (side + 1), 384:448]
        product = dot(left, upper[768 + 64 * side : 768 + 64 * side + 64, :])
        total = product if total is None else total + product
    upper[896:960, :] = total.astype(BF)


def ascend(tops, number, mine, other):
    total = None
    for side in range(2):
        left = tops[RANK * side : RANK * (side + 1), 64 * number : 64 * number + 64]
        rows = slice(HALF * side, HALF * (side + 1))
        product = dot(left, jnp.concatenate([mine[rows], other[rows]], axis=0))
        total = product if total is None else total + product
    return total.astype(BF)


PICKS = (
    (0, 0, 0), (0, 0, 1),
    (32, 1, 0), (32, 1, 1), (32, 1, 2), (32, 1, 3),
    (48, 2, 0), (48, 2, 1),
    (56, 3, 0), (56, 3, 1), (56, 3, 2), (56, 3, 3),
    (60, 4, 0), (60, 4, 1),
)


def lift_kernel(own, near, top_hbm, own_up, near_up, tops, first_top, top_ref, sem):
    copy = pltpu.make_async_copy(top_hbm, top_ref, sem)
    copy.start()
    lift_into(own, own_up)
    lift_into(near, near_up)
    device = lax.axis_index("leaf")
    row, column = iotas(16, 62)
    chosen = jnp.full((16, 62), -1, jnp.int32)
    for number, (begin, shift, flip) in enumerate(PICKS):
        chosen = jnp.where(row == number, begin + ((device >> shift) ^ flip), chosen)
    pick = ones_where(column == chosen)
    copy.wait()
    rows = dot(pick, top_ref[...]).astype(BF)
    tops[...] = dot_nt(rank_order_pair(), tile_rows(regrouped(rows, group_order()))).astype(BF)
    first_top[...] = ascend(tops, 0, own_up[896:960, :], near_up[896:960, :])


def lifted(own, near, top_transfer):
    return pl.pallas_call(
        lift_kernel,
        in_specs=[VMEM_SPEC] * 2 + [HBM_SPEC],
        out_specs=[VMEM_SPEC] * 4,
        out_shape=[
            pltpu.VMEM((960, PROBES), BF),
            pltpu.VMEM((960, PROBES), BF),
            pltpu.VMEM((128, 512), BF),
            pltpu.VMEM((RANK, PROBES), BF),
        ],
        scratch_shapes=[pltpu.VMEM((62, 4096), BF), pltpu.SemaphoreType.DMA],
        compiler_params=limit(6),
        name="lifted",
    )(on_chip(own), on_chip(near), off_chip(top_transfer))


def climb(tops, number, mine, first, second, third):
    def climb_kernel(tops_ref, mine_ref, first_ref, second_ref, third_ref, low_ref, high_ref):
        low = ascend(tops_ref, number, mine_ref[...], first_ref[...])
        side = ascend(tops_ref, number + 1, second_ref[...], third_ref[...])
        low_ref[...] = low
        high_ref[...] = ascend(tops_ref, number + 2, low, side)

    operands = [on_chip(x) for x in (tops, mine, first, second, third)]
    return pl.pallas_call(
        climb_kernel,
        in_specs=[VMEM_SPEC] * 5,
        out_specs=[VMEM_SPEC] * 2,
        out_shape=[pltpu.VMEM((RANK, PROBES), BF)] * 2,
        compiler_params=limit(4),
        name="climb_%d" % number,
    )(*operands)


CHUNK = 96


def place_kernel(sources, tiles_hbm, tail_ref, d0, d1, d2, d3, d4, tiles_ref, spread, sems):
    copies = []
    for k in range(11):
        size = CHUNK if k < 10 else 48
        rows = pl.ds(CHUNK * k, size)
        copies.append(pltpu.make_async_copy(tiles_hbm.at[rows], tiles_ref.at[rows], sems.at[k]))
        copies[-1].start()
    device = lax.axis_index("leaf")
    odd = device & 1

    def slot_of(entry, height):
        shift = 4 - height
        index = sources[entry] - ((device - 2) << shift)
        piece = index >> shift
        piece = jnp.where(odd == 1, 4 - piece, piece)
        piece = jnp.where(
            piece == 2,
            0,
            jnp.where(piece == 3, 1, jnp.where(piece == 4, 2, jnp.where(piece == 1, 3, 4))),
        )
        return (piece << shift) + (index & ((1 << shift) - 1))

    order = group_order()
    eye = identity(128)

    def scatter(first_row, entries):
        for row in range(0, len(entries), 16):
            at = first_row + row
            if not isinstance(at, int):
                at = pl.multiple_of(at, 16)
            if len(entries) - row < 16:
                block = jnp.concatenate([tail_ref[...], jnp.zeros((1, 4096), BF)], axis=0)
            else:
                block = tiles_ref[pl.ds(at, 16), :]
            regroup = regrouped(block, order)
            for e in range(min(16, len(entries) - row)):
                base, height, entry = entries[row + e]
                at = base + slot_of(entry, height)
                spread[at, 0:16, :] = regroup[16 * e : 16 * e + 16, :128]
                spread[at, 16:32, :] = regroup[16 * e : 16 * e + 16, 128:]

    def emit(out, base, count, row):
        for piece in range(5):
            at = base + piece * count
            flat = spread[at : at + count].reshape(count * HALF, 128)
            flip = dot_nt(eye, flat).astype(BF)
            width = count * HALF
            out[piece, pl.ds(row, RANK), 0:width] = flip[:RANK]
            out[piece, pl.ds(row, RANK), width : 2 * width] = flip[RANK:]

    def clear():
        spread[...] = jnp.zeros_like(spread)

    def leaves(k, carry):
        pltpu.make_async_copy(tiles_hbm.at[pl.ds(0, CHUNK)], tiles_ref.at[pl.ds(0, CHUNK)], sems.at[k]).wait()
        base = k * CHUNK
        clear()
        scatter(base, [(80 * (e // 48), 0, base + e) for e in range(CHUNK)])
        for t in range(2):
            emit(d0, 80 * t, 16, pl.multiple_of(k * 128 + RANK * t, RANK))
        return carry

    lax.fori_loop(0, 8, leaves, 0)
    for k in range(8, 10):
        copies[k].wait()
        base = k * CHUNK
        clear()
        scatter(base, [(40 * (e // 24), 1, base + e) for e in range(CHUNK)])
        for t in range(4):
            emit(d1, 40 * t, 8, (k - 8) * 256 + RANK * t)
    copies[10].wait()
    clear()
    entries = [(20 * (e // 12), 2, 960 + e) for e in range(48)]
    entries += [(80 + 10 * (e // 6), 3, 1008 + e) for e in range(12)]
    entries += [(100, 4, 1020 + e) for e in range(3)]
    scatter(960, entries)
    for t in range(4):
        emit(d2, 20 * t, 4, RANK * t)
    for t in range(2):
        emit(d3, 80 + 10 * t, 2, RANK * t)
    emit(d4, 100, 1, 0)


def placed_tiles(sources, couplings):
    return pl.pallas_call(
        place_kernel,
        in_specs=[pl.BlockSpec(memory_space=pltpu.SMEM), HBM_SPEC, VMEM_SPEC],
        out_specs=[VMEM_SPEC] * 5,
        out_shape=[pltpu.VMEM((5, RANK * c, RANK * c), BF) for c in COUNTS],
        scratch_shapes=[
            pltpu.VMEM((1008, 4096), BF),
            pltpu.VMEM((160, HALF, 128), BF),
            pltpu.SemaphoreType.DMA((11,)),
        ],
        compiler_params=limit(14),
        name="placed_tiles",
    )(sources, off_chip(couplings), on_chip(couplings[1008:]))


ROWS = (0, 512, 768, 896)


def iotas(rows, columns):
    shape = (rows, columns)
    return (
        lax.broadcasted_iota(jnp.int32, shape, 0),
        lax.broadcasted_iota(jnp.int32, shape, 1),
    )


def natural(rank):
    return (rank & 31) * 2 + (rank >> 5)


def ones_where(mask):
    return jnp.where(mask, 1.0, 0.0).astype(BF)


def rank_order():
    row, column = iotas(RANK, RANK)
    return ones_where(column == natural(row))


def rank_order_pair():
    row, column = iotas(2 * RANK, 2 * RANK)
    return ones_where(column == (row & 64) + natural(row & 63))


def identity(size):
    row, column = iotas(size, size)
    return ones_where(row == column)


def group_order():
    row, column = iotas(256, 256)
    return ones_where(column == (row & 15) * 16 + (row >> 4))


def dot(left, right):
    return jnp.dot(left, right, preferred_element_type=F32)


def dot_nt(left, right):
    return lax.dot_general(left, right, (((1,), (1,)), ((), ())), preferred_element_type=F32)


def regrouped(block, order):
    halves = [
        jnp.concatenate(
            [block[:, (16 * half + g) * 128 : (16 * half + g + 1) * 128] for g in range(16)], axis=0
        )
        for half in range(2)
    ]
    return dot(order, jnp.concatenate(halves, axis=1)).astype(BF)


def tile_rows(regroup):
    pieces = []
    for entry in range(16):
        rows = slice(16 * entry, 16 * entry + 16)
        pieces.append(regroup[rows, :128])
        pieces.append(regroup[rows, 128:])
    return jnp.concatenate(pieces, axis=0)


def first_kernel(points_hbm, basis_hbm, links_hbm, out_ref, points_ref, basis_ref, links_ref, sems):
    links_copy = pltpu.make_async_copy(links_hbm, links_ref, sems.at[9])
    links_copy.start()
    basis_copy = pltpu.make_async_copy(basis_hbm, basis_ref, sems.at[8])
    basis_copy.start()
    copies = []
    for k in range(8):
        rows = pl.ds(512 * k, 512)
        copies.append(pltpu.make_async_copy(points_hbm.at[rows], points_ref.at[rows], sems.at[k]))
        copies[-1].start()
    order = group_order()
    flip = rank_order_pair()
    ranks = rank_order()
    links_copy.wait()
    high = jnp.concatenate([links_ref[16:30, :], jnp.zeros((2, 4096), BF)], axis=0)
    for number, block in enumerate((links_ref[0:16, :], high)):
        tiles = tile_rows(regrouped(block, order))
        out_ref[1024 + 128 * number : 1152 + 128 * number, :] = dot_nt(flip, tiles).astype(BF)
    basis_copy.wait()
    for k in range(8):
        basis = jnp.concatenate([basis_ref[2 * k], basis_ref[2 * k + 1]], axis=1)
        basis = dot(ranks, basis).astype(BF)
        copies[k].wait()
        for j in range(2):
            at = 512 * k + LEAF * j
            moment = dot(basis[:, LEAF * j : LEAF * (j + 1)], points_ref[at : at + LEAF, :]).astype(BF)
            to = (2 * k + j) * HALF
            out_ref[to : to + HALF, :] = moment[:HALF]
            out_ref[512 + to : 512 + to + HALF, :] = moment[HALF:]


VMEM_SPEC = pl.BlockSpec(memory_space=pltpu.VMEM)
HBM_SPEC = pl.BlockSpec(memory_space=pl.ANY)


def on_chip(value):
    return pltpu.with_memory_space_constraint(value, pltpu.VMEM)


def off_chip(value):
    return pltpu.with_memory_space_constraint(value, pltpu.HBM)


def limit(mebibytes):
    return pltpu.CompilerParams(vmem_limit_bytes=mebibytes << 20)


def first_moments(points, leaf_basis, local_transfer):
    return pl.pallas_call(
        first_kernel,
        in_specs=[HBM_SPEC] * 3,
        out_specs=VMEM_SPEC,
        out_shape=pltpu.VMEM((1280, PROBES), BF),
        scratch_shapes=[
            pltpu.VMEM((4096, PROBES), BF),
            pltpu.VMEM((LEAF_DEV, RANK, LEAF), BF),
            pltpu.VMEM((30, 4096), BF),
            pltpu.SemaphoreType.DMA((10,)),
        ],
        compiler_params=limit(10),
        name="first_moments",
    )(off_chip(points), off_chip(leaf_basis), off_chip(local_transfer))


def lift_into(packet, upper):
    low_side = lax.broadcasted_iota(jnp.int32, (RANK, 128), 1) < 64
    zero = jnp.zeros((RANK, 128), BF)

    def pair_of_targets(links, lanes, source, start, stride):
        total = None
        for side in range(2):
            left = packet[links + RANK * side : links + RANK * (side + 1), lanes : lanes + 128]
            left = jnp.concatenate(
                [jnp.where(low_side, left, zero), jnp.where(low_side, zero, left)], axis=0
            )
            begin = start + stride * side
            product = dot(left, source[begin : begin + 128, :])
            total = product if total is None else total + product
        return total.astype(BF)

    def keep(moment, base, count, first):
        for j in range(2):
            for side in range(2):
                at = base + side * count * HALF + (first + j) * HALF
                upper[at : at + HALF, :] = moment[j * RANK + side * HALF : j * RANK + (side + 1) * HALF]

    for u in range(4):
        keep(pair_of_targets(1024, 128 * u, packet, 128 * u, 512), 0, 8, 2 * u)
    for u in range(2):
        keep(pair_of_targets(1152, 128 * u, upper, 128 * u, 256), 512, 4, 2 * u)
    keep(pair_of_targets(1152, 256, upper, 512, 128), 768, 2, 0)
    total = None
    for side in range(2):
        left = packet[1152 + RANK * side : 1152 + RANK * (side + 1), 384:448]
        product = dot(left, upper[768 + 64 * side : 768 + 64 * side + 64, :])
        total = product if total is None else total + product
    upper[896:960, :] = total.astype(BF)


def ascend(tops, number, mine, other):
    total = None
    for side in range(2):
        left = tops[RANK * side : RANK * (side + 1), 64 * number : 64 * number + 64]
        rows = slice(HALF * side, HALF * (side + 1))
        product = dot(left, jnp.concatenate([mine[rows], other[rows]], axis=0))
        total = product if total is None else total + product
    return total.astype(BF)


PICKS = (
    (0, 0, 0), (0, 0, 1),
    (32, 1, 0), (32, 1, 1), (32, 1, 2), (32, 1, 3),
    (48, 2, 0), (48, 2, 1),
    (56, 3, 0), (56, 3, 1), (56, 3, 2), (56, 3, 3),
    (60, 4, 0), (60, 4, 1),
)


def lift_kernel(own, near, top_hbm, own_up, near_up, tops, first_top, top_ref, sem):
    copy = pltpu.make_async_copy(top_hbm, top_ref, sem)
    copy.start()
    lift_into(own, own_up)
    lift_into(near, near_up)
    device = lax.axis_index("leaf")
    row, column = iotas(16, 62)
    chosen = jnp.full((16, 62), -1, jnp.int32)
    for number, (begin, shift, flip) in enumerate(PICKS):
        chosen = jnp.where(row == number, begin + ((device >> shift) ^ flip), chosen)
    pick = ones_where(column == chosen)
    copy.wait()
    rows = dot(pick, top_ref[...]).astype(BF)
    tops[...] = dot_nt(rank_order_pair(), tile_rows(regrouped(rows, group_order()))).astype(BF)
    first_top[...] = ascend(tops, 0, own_up[896:960, :], near_up[896:960, :])


def lifted(own, near, top_transfer):
    return pl.pallas_call(
        lift_kernel,
        in_specs=[VMEM_SPEC] * 2 + [HBM_SPEC],
        out_specs=[VMEM_SPEC] * 4,
        out_shape=[
            pltpu.VMEM((960, PROBES), BF),
            pltpu.VMEM((960, PROBES), BF),
            pltpu.VMEM((128, 512), BF),
            pltpu.VMEM((RANK, PROBES), BF),
        ],
        scratch_shapes=[pltpu.VMEM((62, 4096), BF), pltpu.SemaphoreType.DMA],
        compiler_params=limit(6),
        name="lifted",
    )(on_chip(own), on_chip(near), off_chip(top_transfer))


def climb(tops, number, mine, first, second, third):
    def climb_kernel(tops_ref, mine_ref, first_ref, second_ref, third_ref, low_ref, high_ref):
        low = ascend(tops_ref, number, mine_ref[...], first_ref[...])
        side = ascend(tops_ref, number + 1, second_ref[...], third_ref[...])
        low_ref[...] = low
        high_ref[...] = ascend(tops_ref, number + 2, low, side)

    operands = [on_chip(x) for x in (tops, mine, first, second, third)]
    return pl.pallas_call(
        climb_kernel,
        in_specs=[VMEM_SPEC] * 5,
        out_specs=[VMEM_SPEC] * 2,
        out_shape=[pltpu.VMEM((RANK, PROBES), BF)] * 2,
        compiler_params=limit(4),
        name="climb_%d" % number,
    )(*operands)


def place_kernel(sources, tiles_ref, d0, d1, d2, d3, d4, spread):
    step = pl.program_id(0)
    device = lax.axis_index("leaf")
    odd = device & 1

    def slot_of(entry, height):
        shift = 4 - height
        index = sources[entry] - ((device - 2) << shift)
        piece = index >> shift
        piece = jnp.where(odd == 1, 4 - piece, piece)
        piece = jnp.where(
            piece == 2,
            0,
            jnp.where(piece == 3, 1, jnp.where(piece == 4, 2, jnp.where(piece == 1, 3, 4))),
        )
        return (piece << shift) + (index & ((1 << shift) - 1))

    order = group_order()
    eye = identity(128)

    def scatter(first_row, entries):
        row = first_row
        while row < first_row + len(entries):
            block = tiles_ref[row : row + 16, :]
            if len(entries) - (row - first_row) < 16:
                keep, _ = iotas(16, 4096)
                block = jnp.where(
                    keep < len(entries) - (row - first_row), block.astype(F32), 0.0
                ).astype(BF)
            regroup = regrouped(block, order)
            for e in range(min(16, len(entries) - (row - first_row))):
                base, height, entry = entries[row - first_row + e]
                at = base + slot_of(entry, height)
                spread[at, 0:16, :] = regroup[16 * e : 16 * e + 16, :128]
                spread[at, 16:32, :] = regroup[16 * e : 16 * e + 16, 128:]
            row += 16

    def flipped(base, count):
        flat = spread[base : base + count].reshape(count * HALF, 128)
        return dot_nt(eye, flat).astype(BF)

    def emit(out, base, count, row):
        for piece in range(5):
            flip = flipped(base + piece * count, count)
            width = count * HALF
            out[piece, row : row + RANK, 0:width] = flip[:RANK]
            out[piece, row : row + RANK, width : 2 * width] = flip[RANK:]

    spread[...] = jnp.zeros_like(spread)

    @pl.when(step < 8)
    def _():
        base = step * 96
        scatter(0, [(80 * (e // 48), 0, base + e) for e in range(96)])
        for t in range(2):
            emit(d0, 80 * t, 16, RANK * t)

    @pl.when((step >= 8) & (step < 10))
    def _():
        base = step * 96
        scatter(0, [(40 * (e // 24), 1, base + e) for e in range(96)])
        for t in range(4):
            emit(d1, 40 * t, 8, RANK * t)

    @pl.when(step == 10)
    def _():
        entries = [(20 * (e // 12), 2, 960 + e) for e in range(48)]
        entries += [(80 + 10 * (e // 6), 3, 1008 + e) for e in range(12)]
        entries += [(100, 4, 1020 + e) for e in range(3)]
        scatter(0, entries)
        for t in range(4):
            emit(d2, 20 * t, 4, RANK * t)
        for t in range(2):
            emit(d3, 80 + 10 * t, 2, RANK * t)
        emit(d4, 100, 1, 0)


def placed_tiles(sources, couplings):
    return pl.pallas_call(
        place_kernel,
        grid_spec=pltpu.PrefetchScalarGridSpec(
            num_scalar_prefetch=1,
            grid=(11,),
            in_specs=[pl.BlockSpec((96, 4096), lambda i, s: (i, 0))],
            out_specs=[
                pl.BlockSpec((5, 128, 1024), lambda i, s: (0, jnp.minimum(i, 7), 0)),
                pl.BlockSpec((5, 256, 512), lambda i, s: (0, jnp.clip(i - 8, 0, 1), 0)),
                pl.BlockSpec((5, 256, 256), lambda i, s: (0, 0, 0)),
                pl.BlockSpec((5, 128, 128), lambda i, s: (0, 0, 0)),
                pl.BlockSpec((5, 64, 64), lambda i, s: (0, 0, 0)),
            ],
            scratch_shapes=[pltpu.VMEM((160, HALF, 128), BF)],
        ),
        out_shape=[
            jax.ShapeDtypeStruct((5, RANK * c, RANK * c), BF) for c in COUNTS
        ],
        name="placed_tiles",
    )(sources, couplings)


ROWS = (0, 1024, 1536, 1792, 1920)


def couple_pieces(total, pieces, dense):
    for height, count in enumerate(COUNTS):
        width = RANK * count
        value = total(height)
        for packet, upper, tile in pieces:
            if height == 0:
                moment = packet[0:1024, :]
            else:
                at = LIFT_ROWS[height - 1]
                moment = upper[at : at + width, :]
            product = dot(dense[height][tile], moment)
            value = product if value is None else value + product
        yield height, width, value


def near_kernel(own, near, own_up, near_up, d0, d1, d2, d3, d4, out):
    pieces = ((own, own_up, 0), (near, near_up, 1))
    for height, width, value in couple_pieces(lambda h: None, pieces, (d0, d1, d2, d3, d4)):
        out[ROWS[height] : ROWS[height] + width, :] = value


def far_kernel(first, second, third, acc, t1, t2, t3, t4, t5, d0, d1, d2, d3, d4, out, tops, up_a, up_b, up_c):
    row, column = iotas(RANK, RANK)
    back = ones_where(natural(column) == row)
    for k, top in enumerate((t1, t2, t3, t4, t5)):
        tops[k] = dot(back, top[...]).astype(BF)
    lift_into(first, up_a)
    lift_into(second, up_b)
    lift_into(third, up_c)
    pieces = ((first, up_a, 2), (second, up_b, 4), (third, up_c, 3))
    start = lambda h: acc[ROWS[h] : ROWS[h] + RANK * COUNTS[h], :]
    for height, width, value in couple_pieces(start, pieces, (d0, d1, d2, d3, d4)):
        out[ROWS[height] : ROWS[height] + width, :] = value.astype(BF)


def couple_near(own, near, own_up, near_up, dense):
    operands = [on_chip(x) for x in (own, near, own_up, near_up, *dense)]
    return pl.pallas_call(
        near_kernel,
        in_specs=[VMEM_SPEC] * 9,
        out_specs=VMEM_SPEC,
        out_shape=pltpu.VMEM((1984, PROBES), F32),
        compiler_params=limit(8),
        name="couple_near",
    )(*operands)


def couple_far(first, second, third, acc, tops, dense):
    operands = [on_chip(x) for x in (first, second, third, acc, *tops, *dense)]
    return pl.pallas_call(
        far_kernel,
        in_specs=[VMEM_SPEC] * 14,
        out_specs=[VMEM_SPEC] * 2,
        out_shape=[
            jax.ShapeDtypeStruct((1984, PROBES), BF),
            jax.ShapeDtypeStruct((5, RANK, PROBES), BF),
        ],
        scratch_shapes=[pltpu.VMEM((960, PROBES), BF)] * 3,
        compiler_params=limit(16),
        name="couple_far",
    )(*operands)


def route(step):
    devices = range(lax.axis_size("leaf"))
    return [(i, step(i)) for i in devices if step(i) in devices]


def sent(block, step):
    return lax.ppermute(block, "leaf", route(step))


def shards(points, leaf_basis, local_transfer, top_transfer, sources, couplings):
    own = first_moments(points, leaf_basis, local_transfer)
    near = sent(own, lambda i: i ^ 1)
    inner = sent(own, lambda i: i + 2 if i % 2 else i - 2)
    outer = sent(own, lambda i: i - 2 if i % 2 else i + 2)
    own_up, near_up, tops, first_top = lifted(own, near, top_transfer)
    over = [sent(first_top, lambda i: i ^ k) for k in (2, 4, 6)]
    couplings, first_top = lax.optimization_barrier((couplings, first_top))
    dense = placed_tiles(sources, couplings)
    over, dense = lax.optimization_barrier((over, dense))
    second_top, third_top = climb(tops, 1, first_top, *over)
    across = [sent(third_top, lambda i: i ^ k) for k in (8, 16, 24)]
    own, third_top = lax.optimization_barrier((own, third_top))
    acc = couple_near(own, near, own_up, near_up, dense)
    inner, outer, across, acc = lax.optimization_barrier((inner, outer, across, acc))
    relayed = sent(inner, lambda i: i ^ 1)
    fourth_top, fifth_top = climb(tops, 4, third_top, *across)
    ladder = (first_top, second_top, third_top, fourth_top, fifth_top)
    coupled, ancestors = couple_far(inner, outer, relayed, acc, ladder, dense)
    return coupled.reshape(31, RANK, PROBES), ancestors[None]


def solution(mesh):
    placed = (
        P("leaf", "probe"),
        P("leaf", None, None),
        P("leaf", None),
        P(),
        P("leaf"),
        P("leaf", None),
    )
    return jax.shard_map(
        shards,
        mesh=mesh,
        in_specs=placed,
        out_specs=(P("leaf", None, "probe"), P("leaf", None, None, "probe")),
        check_vma=False,
    )
```

```python
import functools

import jax
import jax.numpy as jnp
from jax import lax
from jax.experimental import pallas as pl
from jax.experimental.pallas import tpu as pltpu
from jax.sharding import PartitionSpec as P


LEAF = 256
RANK = 64
PROBES = 512
LOCAL = 5
LEAF_DEV = 16
HALF = 32
BF = jnp.bfloat16
F32 = jnp.float32
COUNTS = (16, 8, 4, 2, 1)
LIFT_ROWS = (0, 512, 768, 896)


def iotas(rows, columns):
    shape = (rows, columns)
    return (
        lax.broadcasted_iota(jnp.int32, shape, 0),
        lax.broadcasted_iota(jnp.int32, shape, 1),
    )


def natural(rank):
    return (rank & 31) * 2 + (rank >> 5)


def ones_where(mask):
    return jnp.where(mask, 1.0, 0.0).astype(BF)


def rank_order():
    row, column = iotas(RANK, RANK)
    return ones_where(column == natural(row))


def rank_order_pair():
    row, column = iotas(2 * RANK, 2 * RANK)
    return ones_where(column == (row & 64) + natural(row & 63))


def group_order():
    row, column = iotas(256, 256)
    return ones_where(column == (row & 15) * 16 + (row >> 4))


def dot(left, right):
    return jnp.dot(left, right, preferred_element_type=F32)


def dot_nt(left, right):
    return lax.dot_general(left, right, (((1,), (1,)), ((), ())), preferred_element_type=F32)


def regrouped(block, order):
    halves = [
        jnp.concatenate(
            [block[:, (16 * half + g) * 128 : (16 * half + g + 1) * 128] for g in range(16)], axis=0
        )
        for half in range(2)
    ]
    return dot(order, jnp.concatenate(halves, axis=1)).astype(BF)


def tile_rows(regroup):
    pieces = []
    for entry in range(16):
        rows = slice(16 * entry, 16 * entry + 16)
        pieces.append(regroup[rows, :128])
        pieces.append(regroup[rows, 128:])
    return jnp.concatenate(pieces, axis=0)


def first_kernel(points_hbm, basis_hbm, links_hbm, out_ref, points_ref, basis_ref, links_ref, sems):
    links_copy = pltpu.make_async_copy(links_hbm, links_ref, sems.at[9])
    links_copy.start()
    basis_copy = pltpu.make_async_copy(basis_hbm, basis_ref, sems.at[8])
    basis_copy.start()
    copies = []
    for k in range(8):
        rows = pl.ds(512 * k, 512)
        copies.append(pltpu.make_async_copy(points_hbm.at[rows], points_ref.at[rows], sems.at[k]))
        copies[-1].start()
    order = group_order()
    flip = rank_order_pair()
    ranks = rank_order()
    links_copy.wait()
    high = jnp.concatenate([links_ref[16:30, :], jnp.zeros((2, 4096), BF)], axis=0)
    for number, block in enumerate((links_ref[0:16, :], high)):
        tiles = tile_rows(regrouped(block, order))
        out_ref[1024 + 128 * number : 1152 + 128 * number, :] = dot_nt(flip, tiles).astype(BF)
    basis_copy.wait()
    for k in range(8):
        basis = jnp.concatenate([basis_ref[2 * k], basis_ref[2 * k + 1]], axis=1)
        basis = dot(ranks, basis).astype(BF)
        copies[k].wait()
        for j in range(2):
            at = 512 * k + LEAF * j
            moment = dot(basis[:, LEAF * j : LEAF * (j + 1)], points_ref[at : at + LEAF, :]).astype(BF)
            to = (2 * k + j) * HALF
            out_ref[to : to + HALF, :] = moment[:HALF]
            out_ref[512 + to : 512 + to + HALF, :] = moment[HALF:]


VMEM_SPEC = pl.BlockSpec(memory_space=pltpu.VMEM)
HBM_SPEC = pl.BlockSpec(memory_space=pl.ANY)


def on_chip(value):
    return pltpu.with_memory_space_constraint(value, pltpu.VMEM)


def off_chip(value):
    return pltpu.with_memory_space_constraint(value, pltpu.HBM)


def limit(mebibytes):
    return pltpu.CompilerParams(vmem_limit_bytes=mebibytes << 20)


def first_moments(points, leaf_basis, local_transfer):
    return pl.pallas_call(
        first_kernel,
        in_specs=[HBM_SPEC] * 3,
        out_specs=VMEM_SPEC,
        out_shape=pltpu.VMEM((1280, PROBES), BF),
        scratch_shapes=[
            pltpu.VMEM((4096, PROBES), BF),
            pltpu.VMEM((LEAF_DEV, RANK, LEAF), BF),
            pltpu.VMEM((30, 4096), BF),
            pltpu.SemaphoreType.DMA((10,)),
        ],
        compiler_params=limit(10),
        name="first_moments",
    )(off_chip(points), off_chip(leaf_basis), off_chip(local_transfer))


def lift_into(packet, upper):
    low_side = lax.broadcasted_iota(jnp.int32, (RANK, 128), 1) < 64
    zero = jnp.zeros((RANK, 128), BF)

    def pair_of_targets(links, lanes, source, start, stride):
        total = None
        for side in range(2):
            left = packet[links + RANK * side : links + RANK * (side + 1), lanes : lanes + 128]
            left = jnp.concatenate(
                [jnp.where(low_side, left, zero), jnp.where(low_side, zero, left)], axis=0
            )
            begin = start + stride * side
            product = dot(left, source[begin : begin + 128, :])
            total = product if total is None else total + product
        return total.astype(BF)

    def keep(moment, base, count, first):
        for j in range(2):
            for side in range(2):
                at = base + side * count * HALF + (first + j) * HALF
                upper[at : at + HALF, :] = moment[j * RANK + side * HALF : j * RANK + (side + 1) * HALF]

    for u in range(4):
        keep(pair_of_targets(1024, 128 * u, packet, 128 * u, 512), 0, 8, 2 * u)
    for u in range(2):
        keep(pair_of_targets(1152, 128 * u, upper, 128 * u, 256), 512, 4, 2 * u)
    keep(pair_of_targets(1152, 256, upper, 512, 128), 768, 2, 0)
    total = None
    for side in range(2):
        left = packet[1152 + RANK * side : 1152 + RANK * (side + 1), 384:448]
        product = dot(left, upper[768 + 64 * side : 768 + 64 * side + 64, :])
        total = product if total is None else total + product
    upper[896:960, :] = total.astype(BF)


def ascend(tops, number, mine, other):
    total = None
    for side in range(2):
        left = tops[RANK * side : RANK * (side + 1), 64 * number : 64 * number + 64]
        rows = slice(HALF * side, HALF * (side + 1))
        product = dot(left, jnp.concatenate([mine[rows], other[rows]], axis=0))
        total = product if total is None else total + product
    return total.astype(BF)


PICKS = (
    (0, 0, 0), (0, 0, 1),
    (32, 1, 0), (32, 1, 1), (32, 1, 2), (32, 1, 3),
    (48, 2, 0), (48, 2, 1),
    (56, 3, 0), (56, 3, 1), (56, 3, 2), (56, 3, 3),
    (60, 4, 0), (60, 4, 1),
)


def lift_kernel(own, near, top_hbm, own_up, near_up, tops, first_top, top_ref, sem):
    copy = pltpu.make_async_copy(top_hbm, top_ref, sem)
    copy.start()
    lift_into(own, own_up)
    lift_into(near, near_up)
    device = lax.axis_index("leaf")
    row, column = iotas(16, 62)
    chosen = jnp.full((16, 62), -1, jnp.int32)
    for number, (begin, shift, flip) in enumerate(PICKS):
        chosen = jnp.where(row == number, begin + ((device >> shift) ^ flip), chosen)
    pick = ones_where(column == chosen)
    copy.wait()
    rows = dot(pick, top_ref[...]).astype(BF)
    tops[...] = dot_nt(rank_order_pair(), tile_rows(regrouped(rows, group_order()))).astype(BF)
    first_top[...] = ascend(tops, 0, own_up[896:960, :], near_up[896:960, :])


def lifted(own, near, top_transfer):
    return pl.pallas_call(
        lift_kernel,
        in_specs=[VMEM_SPEC] * 2 + [HBM_SPEC],
        out_specs=[VMEM_SPEC] * 4,
        out_shape=[
            pltpu.VMEM((960, PROBES), BF),
            pltpu.VMEM((960, PROBES), BF),
            pltpu.VMEM((128, 512), BF),
            pltpu.VMEM((RANK, PROBES), BF),
        ],
        scratch_shapes=[pltpu.VMEM((62, 4096), BF), pltpu.SemaphoreType.DMA],
        compiler_params=limit(6),
        name="lifted",
    )(on_chip(own), on_chip(near), off_chip(top_transfer))


def climb(tops, number, mine, first, second, third):
    def climb_kernel(tops_ref, mine_ref, first_ref, second_ref, third_ref, low_ref, high_ref):
        low = ascend(tops_ref, number, mine_ref[...], first_ref[...])
        side = ascend(tops_ref, number + 1, second_ref[...], third_ref[...])
        low_ref[...] = low
        high_ref[...] = ascend(tops_ref, number + 2, low, side)

    operands = [on_chip(x) for x in (tops, mine, first, second, third)]
    return pl.pallas_call(
        climb_kernel,
        in_specs=[VMEM_SPEC] * 5,
        out_specs=[VMEM_SPEC] * 2,
        out_shape=[pltpu.VMEM((RANK, PROBES), BF)] * 2,
        compiler_params=limit(4),
    )(*operands)


CHUNK = 96
SPAN = (0, 11)


def chunk_size(k):
    return CHUNK if k < 10 else 48


def place_kernel(span, sources, tiles_hbm, tail_ref, *refs):
    outs, (tiles_ref, spread_a, spread_b, sems) = refs[:-4], refs[-4:]
    begin, end = span
    for k in range(begin, end):
        size = chunk_size(k)
        pltpu.make_async_copy(
            tiles_hbm.at[pl.ds(CHUNK * k, size)],
            tiles_ref.at[pl.ds(CHUNK * (k - begin), size)],
            sems.at[k - begin],
        ).start()
    device = lax.axis_index("leaf")
    anchors = [(device - 2) << (4 - height) for height in range(LOCAL)]
    order = group_order()

    def scatter(spread, first_row, entries):
        spread[...] = jnp.zeros_like(spread)
        for row in range(0, len(entries), 16):
            at = first_row - CHUNK * begin + row
            if not isinstance(at, int):
                at = pl.multiple_of(at, 16)
            if len(entries) - row < 16:
                block = jnp.where(iotas(16, 4096)[0] < 15, tail_ref[...].astype(F32), 0.0).astype(BF)
            else:
                block = tiles_ref[pl.ds(at, 16), :]
            regroup = regrouped(block, order)
            for e in range(min(16, len(entries) - row)):
                base, height = entries[row + e]
                at = sources[first_row + row + e] - anchors[height] + base
                spread[at, 0:16, :] = regroup[16 * e : 16 * e + 16, :128]
                spread[at, 16:32, :] = regroup[16 * e : 16 * e + 16, 128:]

    def emit(spread, out, base, count, row):
        for piece in range(5):
            at = base + piece * count
            flat = spread[at : at + count].reshape(count * HALF, 128)
            flip = flat.T
            width = count * HALF
            out[piece, pl.ds(row, RANK), 0:width] = flip[:RANK]
            out[piece, pl.ds(row, RANK), width : 2 * width] = flip[RANK:]

    def fill(spread, k):
        if isinstance(k, int) and k == 10:
            entries = [(20 * (e // 12), 2) for e in range(48)]
            entries += [(80 + 10 * (e // 6), 3) for e in range(12)]
            entries += [(100, 4) for _ in range(3)]
        elif isinstance(k, int) and k >= 8:
            entries = [(40 * (e // 24), 1) for e in range(CHUNK)]
        else:
            entries = [(80 * (e // 48), 0) for e in range(CHUNK)]
        rows = pl.ds(0, CHUNK if len(entries) == CHUNK else 48)
        pltpu.make_async_copy(tiles_hbm.at[rows], tiles_ref.at[rows], sems.at[k - begin]).wait()
        scatter(spread, k * CHUNK, entries)

    def drain(spread, k):
        if isinstance(k, int) and k == 10:
            for t in range(4):
                emit(spread, outs[2], 20 * t, 4, RANK * t)
            for t in range(2):
                emit(spread, outs[3], 80 + 10 * t, 2, RANK * t)
            emit(spread, outs[4], 100, 1, 0)
        elif isinstance(k, int) and k >= 8:
            for t in range(4):
                emit(spread, outs[1], 40 * t, 8, (k - 8) * 256 + RANK * t)
        else:
            for t in range(2):
                row = k * 128 + RANK * t
                emit(spread, outs[0], 80 * t, 16, row if isinstance(k, int) else pl.multiple_of(row, RANK))

    def pair(k, carry):
        fill(spread_b, 2 * k + 1)
        drain(spread_a, 2 * k)
        fill(spread_a, 2 * k + 2)
        drain(spread_b, 2 * k + 1)
        return carry

    slots = (spread_a, spread_b)
    fill(spread_a, begin)
    at = begin
    if begin == 0:
        lax.fori_loop(0, 3, pair, 0)
        at = 6
    for k in range(at, end):
        if k + 1 < end:
            fill(slots[(k + 1) % 2], k + 1)
        drain(slots[k % 2], k)


def placed_tiles(sources, couplings, span):
    counts = COUNTS
    rows = sum(chunk_size(k) for k in range(*span))
    return pl.pallas_call(
        functools.partial(place_kernel, span),
        grid=(1,),
        in_specs=[
            pl.BlockSpec(memory_space=pltpu.SMEM),
            HBM_SPEC,
            pl.BlockSpec((16, 4096), lambda i: (63, 0)),
        ],
        out_specs=[VMEM_SPEC] * len(counts),
        out_shape=[pltpu.VMEM((5, RANK * c, RANK * c), BF) for c in counts],
        scratch_shapes=[
            pltpu.VMEM((rows, 4096), BF),
            pltpu.VMEM((160, HALF, 128), BF),
            pltpu.VMEM((160, HALF, 128), BF),
            pltpu.SemaphoreType.DMA((11,)),
        ],
        compiler_params=limit(14),
        name="placed_tiles",
    )(sources, off_chip(couplings), off_chip(couplings))


ROWS = (0, 1024, 1536, 1792, 1920)


def couple_pieces(total, pieces, dense):
    for height, count in enumerate(COUNTS):
        width = RANK * count
        value = total(height)
        for packet, upper, tile in pieces:
            if height == 0:
                moment = packet[0:1024, :]
            else:
                at = LIFT_ROWS[height - 1]
                moment = upper[at : at + width, :]
            product = dot(dense[height][tile], moment)
            value = product if value is None else value + product
        yield height, width, value


def piece_of(step):
    turn = 1 - 2 * (lax.axis_index("leaf") & 1)
    return 2 + turn * step


def middle_kernel(own, near, first, third, own_up, near_up, d0, d1, d2, d3, d4, out, up_a, up_c):
    lift_into(first, up_a)
    lift_into(third, up_c)
    pieces = (
        (own, own_up, 2),
        (near, near_up, piece_of(1)),
        (first, up_a, piece_of(2)),
        (third, up_c, piece_of(-1)),
    )
    for height, width, value in couple_pieces(lambda h: None, pieces, (d0, d1, d2, d3, d4)):
        out[ROWS[height] : ROWS[height] + width, :] = value


def last_kernel(
    packet, acc, t1, t2, t3, t4, t5, d0, d1, d2, d3, d4, out_hbm, tops_hbm, out, tops, up, sems
):
    row, column = iotas(RANK, RANK)
    back = ones_where(natural(column) == row)
    for k, top in enumerate((t1, t2, t3, t4, t5)):
        tops[k] = dot(back, top[...]).astype(BF)
    copies = [pltpu.make_async_copy(tops, tops_hbm, sems.at[5])]
    copies[-1].start()
    piece = piece_of(-2)

    def leave(first, size, number):
        rows = pl.ds(first, size)
        copies.append(pltpu.make_async_copy(out.at[rows], out_hbm.at[rows], sems.at[number]))
        copies[-1].start()

    lift_into(packet, up)
    for block in range(4):
        rows = slice(256 * block, 256 * block + 256)
        product = dot(d0[piece, rows, :], packet[0:1024, :])
        out[rows, :] = (acc[rows, :] + product).astype(BF)
        leave(256 * block, 256, block)
    for height in range(1, LOCAL):
        width = RANK * COUNTS[height]
        rows = slice(ROWS[height], ROWS[height] + width)
        at = LIFT_ROWS[height - 1]
        product = dot((d1, d2, d3, d4)[height - 1][piece], up[at : at + width, :])
        out[rows, :] = (acc[rows, :] + product).astype(BF)
    leave(1024, 960, 4)
    for copy in copies:
        copy.wait()


def couple_middle(own, near, first, third, own_up, near_up, dense):
    operands = [on_chip(x) for x in (own, near, first, third, own_up, near_up, *dense)]
    return pl.pallas_call(
        middle_kernel,
        in_specs=[VMEM_SPEC] * 11,
        out_specs=VMEM_SPEC,
        out_shape=pltpu.VMEM((1984, PROBES), F32),
        scratch_shapes=[pltpu.VMEM((960, PROBES), BF)] * 2,
        compiler_params=limit(8),
        name="couple_middle",
    )(*operands)


def couple_last(packet, acc, tops, dense):
    operands = [on_chip(x) for x in (packet, acc, *tops, *dense)]
    return pl.pallas_call(
        last_kernel,
        in_specs=[VMEM_SPEC] * 12,
        out_specs=[HBM_SPEC] * 2,
        out_shape=[
            pltpu.HBM((1984, PROBES), BF),
            pltpu.HBM((5, RANK, PROBES), BF),
        ],
        scratch_shapes=[
            pltpu.VMEM((1984, PROBES), BF),
            pltpu.VMEM((5, RANK, PROBES), BF),
            pltpu.VMEM((960, PROBES), BF),
            pltpu.SemaphoreType.DMA((6,)),
        ],
        compiler_params=limit(8),
        name="couple_last",
    )(*operands)


def route(step):
    devices = range(lax.axis_size("leaf"))
    return [(i, step(i)) for i in devices if step(i) in devices]


def sent(block, step):
    return lax.ppermute(block, "leaf", route(step))


def tied(*values):
    return lax.optimization_barrier(values)


def whole(points, leaf_basis, local_transfer, top_transfer, sources, couplings):
    own = first_moments(points, leaf_basis, local_transfer)
    near = sent(own, lambda i: i ^ 1)
    inner = sent(own, lambda i: i + 2 if i % 2 else i - 2)
    own_up, near_up, tops, first_top = lifted(own, near, top_transfer)
    over = [sent(first_top, lambda i: i ^ k) for k in (2, 4, 6)]
    couplings, first_top = tied(couplings, first_top)
    dense = placed_tiles(sources, couplings, SPAN)
    late, *dense = tied(own, *dense)
    outer = sent(late, lambda i: i - 2 if i % 2 else i + 2)
    relayed = sent(inner, lambda i: i ^ 1)
    over, dense = tied(over, dense)
    second_top, third_top = climb(tops, 1, first_top, *over)
    across = [sent(third_top, lambda i: i ^ k) for k in (8, 16, 24)]
    own, relayed, third_top = tied(own, relayed, third_top)
    acc = couple_middle(own, near, inner, relayed, own_up, near_up, dense)
    outer, across, acc = tied(outer, across, acc)
    fourth_top, fifth_top = climb(tops, 4, third_top, *across)
    ladder = (first_top, second_top, third_top, fourth_top, fifth_top)
    coupled, ancestors = couple_last(outer, acc, ladder, dense)
    return coupled.reshape(31, RANK, PROBES), ancestors[None]


def solution(mesh):
    placed = (
        P("leaf", "probe"),
        P("leaf", None, None),
        P("leaf", None),
        P(),
        P("leaf"),
        P("leaf", None),
    )
    return jax.shard_map(
        whole,
        mesh=mesh,
        in_specs=placed,
        out_specs=(P("leaf", None, "probe"), P("leaf", None, None, "probe")),
        check_vma=False,
    )
```

```python
import functools

import jax
import jax.numpy as jnp
from jax import lax
from jax.experimental import pallas as pl
from jax.experimental.pallas import tpu as pltpu
from jax.sharding import PartitionSpec as P


LEAF = 256
RANK = 64
PROBES = 512
LOCAL = 5
LEAF_DEV = 16
HALF = 32
BF = jnp.bfloat16
F32 = jnp.float32
COUNTS = (16, 8, 4, 2, 1)
LIFT_ROWS = (0, 512, 768, 896)


def iotas(rows, columns):
    shape = (rows, columns)
    return (
        lax.broadcasted_iota(jnp.int32, shape, 0),
        lax.broadcasted_iota(jnp.int32, shape, 1),
    )


def natural(rank):
    return (rank & 31) * 2 + (rank >> 5)


def ones_where(mask):
    return jnp.where(mask, 1.0, 0.0).astype(BF)


def rank_order():
    row, column = iotas(RANK, RANK)
    return ones_where(column == natural(row))


def rank_order_pair():
    row, column = iotas(2 * RANK, 2 * RANK)
    return ones_where(column == (row & 64) + natural(row & 63))


def group_order():
    row, column = iotas(256, 256)
    return ones_where(column == (row & 15) * 16 + (row >> 4))


def dot(left, right):
    return jnp.dot(left, right, preferred_element_type=F32)


def dot_nt(left, right):
    return lax.dot_general(left, right, (((1,), (1,)), ((), ())), preferred_element_type=F32)


def regrouped(block, order):
    halves = [
        jnp.concatenate(
            [block[:, (16 * half + g) * 128 : (16 * half + g + 1) * 128] for g in range(16)], axis=0
        )
        for half in range(2)
    ]
    return dot(order, jnp.concatenate(halves, axis=1)).astype(BF)


def tile_rows(regroup):
    pieces = []
    for entry in range(16):
        rows = slice(16 * entry, 16 * entry + 16)
        pieces.append(regroup[rows, :128])
        pieces.append(regroup[rows, 128:])
    return jnp.concatenate(pieces, axis=0)


def first_kernel(points_hbm, basis_hbm, links_hbm, out_ref, points_ref, basis_ref, links_ref, sems):
    links_copy = pltpu.make_async_copy(links_hbm, links_ref, sems.at[9])
    links_copy.start()
    basis_copy = pltpu.make_async_copy(basis_hbm, basis_ref, sems.at[8])
    basis_copy.start()
    copies = []
    for k in range(8):
        rows = pl.ds(512 * k, 512)
        copies.append(pltpu.make_async_copy(points_hbm.at[rows], points_ref.at[rows], sems.at[k]))
        copies[-1].start()
    order = group_order()
    flip = rank_order_pair()
    ranks = rank_order()
    links_copy.wait()
    high = jnp.concatenate([links_ref[16:30, :], jnp.zeros((2, 4096), BF)], axis=0)
    for number, block in enumerate((links_ref[0:16, :], high)):
        tiles = tile_rows(regrouped(block, order))
        out_ref[1024 + 128 * number : 1152 + 128 * number, :] = dot_nt(flip, tiles).astype(BF)
    basis_copy.wait()
    for k in range(8):
        basis = jnp.concatenate([basis_ref[2 * k], basis_ref[2 * k + 1]], axis=1)
        basis = dot(ranks, basis).astype(BF)
        copies[k].wait()
        for j in range(2):
            at = 512 * k + LEAF * j
            moment = dot(basis[:, LEAF * j : LEAF * (j + 1)], points_ref[at : at + LEAF, :]).astype(BF)
            to = (2 * k + j) * HALF
            out_ref[to : to + HALF, :] = moment[:HALF]
            out_ref[512 + to : 512 + to + HALF, :] = moment[HALF:]


VMEM_SPEC = pl.BlockSpec(memory_space=pltpu.VMEM)
HBM_SPEC = pl.BlockSpec(memory_space=pl.ANY)


def on_chip(value):
    return pltpu.with_memory_space_constraint(value, pltpu.VMEM)


def off_chip(value):
    return pltpu.with_memory_space_constraint(value, pltpu.HBM)


def limit(mebibytes):
    return pltpu.CompilerParams(vmem_limit_bytes=mebibytes << 20)


def first_moments(points, leaf_basis, local_transfer):
    return pl.pallas_call(
        first_kernel,
        in_specs=[HBM_SPEC] * 3,
        out_specs=VMEM_SPEC,
        out_shape=pltpu.VMEM((1280, PROBES), BF),
        scratch_shapes=[
            pltpu.VMEM((4096, PROBES), BF),
            pltpu.VMEM((LEAF_DEV, RANK, LEAF), BF),
            pltpu.VMEM((30, 4096), BF),
            pltpu.SemaphoreType.DMA((10,)),
        ],
        compiler_params=limit(10),
        name="first_moments",
    )(off_chip(points), off_chip(leaf_basis), off_chip(local_transfer))


def lift_into(packet, upper):
    low_side = lax.broadcasted_iota(jnp.int32, (RANK, 128), 1) < 64
    zero = jnp.zeros((RANK, 128), BF)

    def pair_of_targets(links, lanes, source, start, stride):
        total = None
        for side in range(2):
            left = packet[links + RANK * side : links + RANK * (side + 1), lanes : lanes + 128]
            left = jnp.concatenate(
                [jnp.where(low_side, left, zero), jnp.where(low_side, zero, left)], axis=0
            )
            begin = start + stride * side
            product = dot(left, source[begin : begin + 128, :])
            total = product if total is None else total + product
        return total.astype(BF)

    def keep(moment, base, count, first):
        for j in range(2):
            for side in range(2):
                at = base + side * count * HALF + (first + j) * HALF
                upper[at : at + HALF, :] = moment[j * RANK + side * HALF : j * RANK + (side + 1) * HALF]

    for u in range(4):
        keep(pair_of_targets(1024, 128 * u, packet, 128 * u, 512), 0, 8, 2 * u)
    for u in range(2):
        keep(pair_of_targets(1152, 128 * u, upper, 128 * u, 256), 512, 4, 2 * u)
    keep(pair_of_targets(1152, 256, upper, 512, 128), 768, 2, 0)
    total = None
    for side in range(2):
        left = packet[1152 + RANK * side : 1152 + RANK * (side + 1), 384:448]
        product = dot(left, upper[768 + 64 * side : 768 + 64 * side + 64, :])
        total = product if total is None else total + product
    upper[896:960, :] = total.astype(BF)


def ascend(tops, number, mine, other):
    total = None
    for side in range(2):
        left = tops[RANK * side : RANK * (side + 1), 64 * number : 64 * number + 64]
        rows = slice(HALF * side, HALF * (side + 1))
        product = dot(left, jnp.concatenate([mine[rows], other[rows]], axis=0))
        total = product if total is None else total + product
    return total.astype(BF)


PICKS = (
    (0, 0, 0), (0, 0, 1),
    (32, 1, 0), (32, 1, 1), (32, 1, 2), (32, 1, 3),
    (48, 2, 0), (48, 2, 1),
    (56, 3, 0), (56, 3, 1), (56, 3, 2), (56, 3, 3),
    (60, 4, 0), (60, 4, 1),
)


def lift_kernel(own, near, top_hbm, own_up, near_up, tops, first_top, top_ref, sem):
    copy = pltpu.make_async_copy(top_hbm, top_ref, sem)
    copy.start()
    lift_into(own, own_up)
    lift_into(near, near_up)
    device = lax.axis_index("leaf")
    row, column = iotas(16, 62)
    chosen = jnp.full((16, 62), -1, jnp.int32)
    for number, (begin, shift, flip) in enumerate(PICKS):
        chosen = jnp.where(row == number, begin + ((device >> shift) ^ flip), chosen)
    pick = ones_where(column == chosen)
    copy.wait()
    rows = dot(pick, top_ref[...]).astype(BF)
    tops[...] = dot_nt(rank_order_pair(), tile_rows(regrouped(rows, group_order()))).astype(BF)
    first_top[...] = ascend(tops, 0, own_up[896:960, :], near_up[896:960, :])


def lifted(own, near, top_transfer):
    return pl.pallas_call(
        lift_kernel,
        in_specs=[VMEM_SPEC] * 2 + [HBM_SPEC],
        out_specs=[VMEM_SPEC] * 4,
        out_shape=[
            pltpu.VMEM((960, PROBES), BF),
            pltpu.VMEM((960, PROBES), BF),
            pltpu.VMEM((128, 512), BF),
            pltpu.VMEM((RANK, PROBES), BF),
        ],
        scratch_shapes=[pltpu.VMEM((62, 4096), BF), pltpu.SemaphoreType.DMA],
        compiler_params=limit(6),
        name="lifted",
    )(on_chip(own), on_chip(near), off_chip(top_transfer))


def climb(tops, number, mine, first, second, third):
    def climb_kernel(tops_ref, mine_ref, first_ref, second_ref, third_ref, low_ref, high_ref):
        low = ascend(tops_ref, number, mine_ref[...], first_ref[...])
        side = ascend(tops_ref, number + 1, second_ref[...], third_ref[...])
        low_ref[...] = low
        high_ref[...] = ascend(tops_ref, number + 2, low, side)

    operands = [on_chip(x) for x in (tops, mine, first, second, third)]
    return pl.pallas_call(
        climb_kernel,
        in_specs=[VMEM_SPEC] * 5,
        out_specs=[VMEM_SPEC] * 2,
        out_shape=[pltpu.VMEM((RANK, PROBES), BF)] * 2,
        compiler_params=limit(4),
    )(*operands)


CHUNK = 96
SPAN = (0, 11)


def chunk_size(k):
    return CHUNK if k < 10 else 48


def crowned(tops, first, second, third, others):
    def crown_kernel(tops_ref, t1, t2, t3, other_a, other_b, other_c, out_ref):
        row, column = iotas(RANK, RANK)
        back = ones_where(natural(column) == row)
        fourth = ascend(tops_ref, 4, t3[...], other_a[...])
        side = ascend(tops_ref, 5, other_b[...], other_c[...])
        fifth = ascend(tops_ref, 6, fourth, side)
        for k, top in enumerate((t1[...], t2[...], t3[...], fourth, fifth)):
            out_ref[k] = dot(back, top).astype(BF)

    operands = [on_chip(x) for x in (tops, first, second, third, *others)]
    return pl.pallas_call(
        crown_kernel,
        in_specs=[VMEM_SPEC] * 7,
        out_specs=VMEM_SPEC,
        out_shape=jax.ShapeDtypeStruct((5, RANK, PROBES), BF),
        compiler_params=limit(4),
        name="crown",
    )(*operands)


def place_kernel(span, sources, tiles_hbm, tail_ref, *refs):
    outs, (tiles_ref, spread_a, spread_b, sems) = refs[:-4], refs[-4:]
    begin, end = span
    for k in range(begin, end):
        size = chunk_size(k)
        pltpu.make_async_copy(
            tiles_hbm.at[pl.ds(CHUNK * k, size)],
            tiles_ref.at[pl.ds(CHUNK * (k - begin), size)],
            sems.at[k - begin],
        ).start()
    device = lax.axis_index("leaf")
    anchors = [(device - 2) << (4 - height) for height in range(LOCAL)]
    order = group_order()

    def scatter(spread, first_row, entries):
        spread[...] = jnp.zeros_like(spread)
        for row in range(0, len(entries), 16):
            at = first_row - CHUNK * begin + row
            if not isinstance(at, int):
                at = pl.multiple_of(at, 16)
            if len(entries) - row < 16:
                block = jnp.where(iotas(16, 4096)[0] < 15, tail_ref[...].astype(F32), 0.0).astype(BF)
            else:
                block = tiles_ref[pl.ds(at, 16), :]
            regroup = regrouped(block, order)
            for e in range(min(16, len(entries) - row)):
                base, height = entries[row + e]
                at = sources[first_row + row + e] - anchors[height] + base
                spread[at, 0:16, :] = regroup[16 * e : 16 * e + 16, :128]
                spread[at, 16:32, :] = regroup[16 * e : 16 * e + 16, 128:]

    def emit(spread, out, base, count, row):
        for piece in range(5):
            at = base + piece * count
            flat = spread[at : at + count].reshape(count * HALF, 128)
            flip = flat.T
            width = count * HALF
            out[piece, pl.ds(row, RANK), 0:width] = flip[:RANK]
            out[piece, pl.ds(row, RANK), width : 2 * width] = flip[RANK:]

    def fill(spread, k):
        if isinstance(k, int) and k == 10:
            entries = [(20 * (e // 12), 2) for e in range(48)]
            entries += [(80 + 10 * (e // 6), 3) for e in range(12)]
            entries += [(100, 4) for _ in range(3)]
        elif isinstance(k, int) and k >= 8:
            entries = [(40 * (e // 24), 1) for e in range(CHUNK)]
        else:
            entries = [(80 * (e // 48), 0) for e in range(CHUNK)]
        rows = pl.ds(0, CHUNK if len(entries) == CHUNK else 48)
        pltpu.make_async_copy(tiles_hbm.at[rows], tiles_ref.at[rows], sems.at[k - begin]).wait()
        scatter(spread, k * CHUNK, entries)

    def drain(spread, k):
        if isinstance(k, int) and k == 10:
            for t in range(4):
                emit(spread, outs[2], 20 * t, 4, RANK * t)
            for t in range(2):
                emit(spread, outs[3], 80 + 10 * t, 2, RANK * t)
            emit(spread, outs[4], 100, 1, 0)
        elif isinstance(k, int) and k >= 8:
            for t in range(4):
                emit(spread, outs[1], 40 * t, 8, (k - 8) * 256 + RANK * t)
        else:
            for t in range(2):
                row = k * 128 + RANK * t
                emit(spread, outs[0], 80 * t, 16, row if isinstance(k, int) else pl.multiple_of(row, RANK))

    def pair(k, carry):
        fill(spread_b, 2 * k + 1)
        drain(spread_a, 2 * k)
        fill(spread_a, 2 * k + 2)
        drain(spread_b, 2 * k + 1)
        return carry

    slots = (spread_a, spread_b)
    fill(spread_a, begin)
    at = begin
    if begin == 0:
        lax.fori_loop(0, 3, pair, 0)
        at = 6
    for k in range(at, end):
        if k + 1 < end:
            fill(slots[(k + 1) % 2], k + 1)
        drain(slots[k % 2], k)


def placed_tiles(sources, couplings, span):
    counts = COUNTS
    rows = sum(chunk_size(k) for k in range(*span))
    return pl.pallas_call(
        functools.partial(place_kernel, span),
        grid=(1,),
        in_specs=[
            pl.BlockSpec(memory_space=pltpu.SMEM),
            HBM_SPEC,
            pl.BlockSpec((16, 4096), lambda i: (63, 0)),
        ],
        out_specs=[VMEM_SPEC] * len(counts),
        out_shape=[pltpu.VMEM((5, RANK * c, RANK * c), BF) for c in counts],
        scratch_shapes=[
            pltpu.VMEM((rows, 4096), BF),
            pltpu.VMEM((160, HALF, 128), BF),
            pltpu.VMEM((160, HALF, 128), BF),
            pltpu.SemaphoreType.DMA((11,)),
        ],
        compiler_params=limit(14),
        name="placed_tiles",
    )(sources, off_chip(couplings), off_chip(couplings))


ROWS = (0, 1024, 1536, 1792, 1920)


def couple_pieces(total, pieces, dense):
    for height, count in enumerate(COUNTS):
        width = RANK * count
        value = total(height)
        for packet, upper, tile in pieces:
            if height == 0:
                moment = packet[0:1024, :]
            else:
                at = LIFT_ROWS[height - 1]
                moment = upper[at : at + width, :]
            product = dot(dense[height][tile], moment)
            value = product if value is None else value + product
        yield height, width, value


def piece_of(step):
    turn = 1 - 2 * (lax.axis_index("leaf") & 1)
    return 2 + turn * step


def middle_kernel(own, near, first, third, own_up, near_up, d0, d1, d2, d3, d4, out, up_a, up_c):
    lift_into(first, up_a)
    lift_into(third, up_c)
    pieces = (
        (own, own_up, 2),
        (near, near_up, piece_of(1)),
        (first, up_a, piece_of(2)),
        (third, up_c, piece_of(-1)),
    )
    for height, width, value in couple_pieces(lambda h: None, pieces, (d0, d1, d2, d3, d4)):
        out[ROWS[height] : ROWS[height] + width, :] = value


def last_kernel(
    packet, acc, d0, d1, d2, d3, d4, out_hbm, out, up, sems
):
    copies = []
    piece = piece_of(-2)

    def leave(first, size, number):
        rows = pl.ds(first, size)
        copies.append(pltpu.make_async_copy(out.at[rows], out_hbm.at[rows], sems.at[number]))
        copies[-1].start()

    lift_into(packet, up)
    for block in range(4):
        rows = slice(256 * block, 256 * block + 256)
        product = dot(d0[piece, rows, :], packet[0:1024, :])
        out[rows, :] = (acc[rows, :] + product).astype(BF)
        leave(256 * block, 256, block)
    for height in range(1, LOCAL):
        width = RANK * COUNTS[height]
        rows = slice(ROWS[height], ROWS[height] + width)
        at = LIFT_ROWS[height - 1]
        product = dot((d1, d2, d3, d4)[height - 1][piece], up[at : at + width, :])
        out[rows, :] = (acc[rows, :] + product).astype(BF)
    leave(1024, 960, 4)
    for copy in copies:
        copy.wait()


def couple_middle(own, near, first, third, own_up, near_up, dense):
    operands = [on_chip(x) for x in (own, near, first, third, own_up, near_up, *dense)]
    return pl.pallas_call(
        middle_kernel,
        in_specs=[VMEM_SPEC] * 11,
        out_specs=VMEM_SPEC,
        out_shape=pltpu.VMEM((1984, PROBES), F32),
        scratch_shapes=[pltpu.VMEM((960, PROBES), BF)] * 2,
        compiler_params=limit(8),
        name="couple_middle",
    )(*operands)


def couple_last(packet, acc, dense):
    operands = [on_chip(x) for x in (packet, acc, *dense)]
    return pl.pallas_call(
        last_kernel,
        in_specs=[VMEM_SPEC] * 7,
        out_specs=HBM_SPEC,
        out_shape=pltpu.HBM((1984, PROBES), BF),
        scratch_shapes=[
            pltpu.VMEM((1984, PROBES), BF),
            pltpu.VMEM((960, PROBES), BF),
            pltpu.SemaphoreType.DMA((5,)),
        ],
        compiler_params=limit(8),
        name="couple_last",
    )(*operands)


def route(step):
    devices = range(lax.axis_size("leaf"))
    return [(i, step(i)) for i in devices if step(i) in devices]


def sent(block, step):
    return lax.ppermute(block, "leaf", route(step))


def tied(*values):
    return lax.optimization_barrier(values)


def whole(points, leaf_basis, local_transfer, top_transfer, sources, couplings):
    own = first_moments(points, leaf_basis, local_transfer)
    near = sent(own, lambda i: i ^ 1)
    inner = sent(own, lambda i: i + 2 if i % 2 else i - 2)
    own_up, near_up, tops, first_top = lifted(own, near, top_transfer)
    over = [sent(first_top, lambda i: i ^ k) for k in (2, 4, 6)]
    couplings, first_top = tied(couplings, first_top)
    dense = placed_tiles(sources, couplings, SPAN)
    late, *dense = tied(own, *dense)
    outer = sent(late, lambda i: i - 2 if i % 2 else i + 2)
    relayed = sent(inner, lambda i: i ^ 1)
    over, dense = tied(over, dense)
    second_top, third_top = climb(tops, 1, first_top, *over)
    across = [sent(third_top, lambda i: i ^ k) for k in (8, 16, 24)]
    own, relayed, third_top = tied(own, relayed, third_top)
    acc = couple_middle(own, near, inner, relayed, own_up, near_up, dense)
    outer, acc = tied(outer, acc)
    coupled = couple_last(outer, acc, dense)
    across, coupled = tied(across, coupled)
    ancestors = crowned(tops, first_top, second_top, third_top, across)
    return coupled.reshape(31, RANK, PROBES), ancestors[None]


def solution(mesh):
    placed = (
        P("leaf", "probe"),
        P("leaf", None, None),
        P("leaf", None),
        P(),
        P("leaf"),
        P("leaf", None),
    )
    return jax.shard_map(
        whole,
        mesh=mesh,
        in_specs=placed,
        out_specs=(P("leaf", None, "probe"), P("leaf", None, None, "probe")),
        check_vma=False,
    )
```
